512 devices in a mesh: dp: 64 (over y, z), tensor: 8 (over x, core).
Axes of the slice: x: 4, y: 4, z: 16, core: 2. Of those that a mesh axis runs over, the one named last changes fastest.
Arguments:
- grad_kv: bfloat16 [64, 2, 512, 2048], P('dp', None, 'tensor'), may hold values from -16 to 16
- error_kv: bfloat16 [64, 2, 512, 2048], P('dp', None, 'tensor'), may hold values from -4 to 4
- moment_kv: bfloat16 [64, 2, 512, 2048], P('dp', None, 'tensor'), may hold values from -6 to 6
- start_dirs: float32 [2, 32, 2048], replicated, may hold values from -6 to 6
- weight_kv: float32 [2, 512, 2048], P(None, 'tensor', 'dp'), may hold values from -6 to 6
- norm_grads: bfloat16 [64, 2, 2048], P('dp', None, 'tensor'), may hold values from -16 to 16
- norm_gains: float32 [2, 8, 256], P(None, 'tensor', 'dp'), may hold values from 0.5 to 1.5
Outputs:
- new_weight_kv: float32 [2, 512, 2048], P(None, 'tensor', 'dp')
- new_error_kv: bfloat16 [64, 2, 512, 2048], P('dp', None, 'tensor')
- new_moment_kv: bfloat16 [64, 2, 512, 2048], P('dp', None, 'tensor')
- new_gains: float32 [2, 8, 256], P(None, 'tensor', 'dp')
The draws below stay inside these ranges and needn't reach their ends.
All inputs are finite; a program needn't handle non-finite values.
Results may differ from the reference program's by a relative error of at most 0.001.
Values sent between devices are 32-bit elements; how exact they have to be, the bound alone decides.
No kernel may reach another device: no remote copies, remote signals or barrier semaphores. Data moves between devices by JAX's collectives and lax.ppermute only.
A program may use at most 64 MiB of HBM per device.

```python
import jax
import jax.numpy as jnp
from jax import lax

D = 2048
KVW = 512
RANK = 32
ROUNDS = 2
REPLICAS = 64
N_TENSOR = 8


def spiked(result, stream_key, source, target, blocks, factor):
    owner, partner = [(jnp.arange(result.shape[position]) // (result.shape[position] // blocks)).reshape([-1 if axis == position else 1 for axis in range(result.ndim)]) for position in (source, target)]
    chosen = jax.random.permutation(stream_key, blocks)[partner]
    strong = (owner == chosen) | (owner == (partner + blocks // 2) % blocks)
    return jnp.where(strong, factor * result, result)


def steps_of(rng, extent, pieces, smallest, high):
    gain, own = 1.0, jax.random.fold_in(rng, 6)
    for dim, blocks in pieces:
        draws = jnp.exp(jax.random.uniform(jax.random.fold_in(own, dim), (blocks,), jnp.float32, smallest / len(pieces), high / len(pieces)))
        gain = gain * jnp.repeat(draws, extent[dim] // blocks).reshape([-1 if axis == dim else 1 for axis in range(len(extent))])
    return gain


def bell_draw(rng, dims, deviation, reach, pieces=(), kind=jnp.bfloat16):
    result = jax.random.normal(rng, dims, jnp.float32) * deviation
    if len(pieces) > 0:
        result = steps_of(rng, dims, pieces, -0.22, 0.18) * result
    return jnp.clip(result, min=-reach, max=reach).astype(kind)


def gaussian_with(rng, extent, deviation, reach, cuts, heavy, kind=jnp.bfloat16):
    drawn = deviation * jax.random.normal(rng, extent, jnp.float32)
    if cuts:
        drawn = drawn * steps_of(rng, extent, cuts, -0.22, 0.18)
    return jnp.clip(spiked(drawn, jax.random.fold_in(rng, 3), *heavy), -reach, reach).astype(kind)


def setup_inputs(seed: int = 0) -> dict:
    arg_keys = jax.random.split(jax.random.key(seed), 8)
    return {
        "grad_kv": gaussian_with(arg_keys[0], (REPLICAS, 2, KVW, D), 1.0, 16.0, ((0, 64), (2, 8)), (0, 3, 64, 4.0)),
        "error_kv": bell_draw(arg_keys[1], (REPLICAS, 2, KVW, D), 0.5, 4.0, ((0, 64), (2, 8))),
        "moment_kv": bell_draw(arg_keys[2], (REPLICAS, 2, KVW, D), 1.0, 6.0, ((0, 64), (2, 8))),
        "start_dirs": bell_draw(arg_keys[3], (2, RANK, D), 1.0, 6.0, (), jnp.float32),
        "weight_kv": bell_draw(arg_keys[4], (2, KVW, D), 1.0, 6.0, ((1, 8), (2, 64)), jnp.float32),
        "norm_grads": gaussian_with(arg_keys[5], (REPLICAS, 2, D), 1.0, 16.0, ((0, 64), (2, 8)), (0, 2, 64, 4.0)),
        "norm_gains": jnp.clip(1.0 + 0.1 * jax.random.normal(arg_keys[6], (2, N_TENSOR, D // N_TENSOR), jnp.float32), 0.5, 1.5),
    }


momentum_decay = 0.9
step_size = 0.5

def tri_solve(triangle, columns):
    return jax.scipy.linalg.solve_triangular(triangle, columns, lower=True)

def orthonormal(factor):
    gram_matrix = jnp.einsum('mrk,mrj->mkj', factor, factor, precision=lax.Precision.HIGHEST)
    cholesky_factor = jnp.linalg.cholesky(gram_matrix)
    solved = jax.vmap(tri_solve)(cholesky_factor, jnp.swapaxes(factor, 1, 2))
    return jnp.swapaxes(solved, 1, 2)

def reference(grad_kv, error_kv, moment_kv, start_dirs, weight_kv, norm_grads, norm_gains):
    moment_f = momentum_decay * moment_kv.astype(jnp.float32) + grad_kv.astype(jnp.float32)
    new_moment_kv = moment_f.astype(jnp.bfloat16)
    inputs = moment_f + error_kv.astype(jnp.float32)
    directions = start_dirs.astype(jnp.float32)
    basis = None
    for step in range(ROUNDS):
        factor = jnp.einsum('nmrd,mkd->mrk', inputs, directions, precision=lax.Precision.HIGHEST)
        basis = orthonormal(factor)
        directions = jnp.einsum('nmrd,mrk->mkd', inputs, basis, precision=lax.Precision.HIGHEST)
    approx = jnp.einsum('mrk,mkd->mrd', basis, directions, precision=lax.Precision.HIGHEST) / REPLICAS
    new_error_kv = (inputs - approx[None]).astype(jnp.bfloat16)
    new_weight_kv = weight_kv - step_size * approx
    mean_norm = jnp.sum(norm_grads.astype(jnp.float32), axis=0) / REPLICAS
    gains_flat = norm_gains.reshape(2, D)
    new_gains = (gains_flat - step_size * mean_norm).reshape(2, N_TENSOR, D // N_TENSOR)
    return (new_weight_kv, new_error_kv, new_moment_kv, new_gains)
```

```python
import jax
import jax.numpy as jnp
from jax import lax
from jax.sharding import Mesh
from jax.sharding import PartitionSpec as P

momentum_decay = 0.9
step_size = 0.5
Y_CHIPS = 4
CORES = 2
HIGH = lax.Precision.HIGHEST


def spread(value, axes, count):
    copies = jnp.broadcast_to(value[None], (count,) + value.shape)
    return lax.all_to_all(copies, axes, 0, 0, tiled=True)


def tri_solve(triangle, columns):
    return jax.scipy.linalg.solve_triangular(triangle, columns, lower=True)


def pack(product, gram):
    parts = (product[0], product[1], gram[0], gram[1])
    joined = jnp.concatenate(parts, axis=1)
    return jnp.pad(joined, ((0, 0), (0, -joined.shape[1] % 128)))


def shards(grad_kv, error_kv, moment_kv, start_dirs, weight_kv, norm_grads, norm_gains):
    n_y, n_z, n_x, n_core = (lax.axis_size(a) for a in ("y", "z", "x", "core"))
    replicas = n_y * n_z
    y, z, core = (lax.axis_index(a) for a in ("y", "z", "core"))
    _, n_mat, rows, width = grad_kv.shape
    rank = start_dirs.shape[1]
    groups = n_y * n_core
    cols = width // groups
    chip_rows = rows * n_core
    z_rows = chip_rows // n_z
    features = norm_grads.shape[2] // n_y
    gain_cols = norm_gains.shape[2]

    moment_f = momentum_decay * moment_kv.astype(jnp.float32) + grad_kv.astype(jnp.float32)
    new_moment_kv = moment_f.astype(jnp.bfloat16)
    inputs = (moment_f + error_kv.astype(jnp.float32))[0]

    own_factor = jnp.einsum("mrd,mkd->rmk", inputs, start_dirs, precision=HIGH).reshape(rows, n_mat * rank)
    blocks = inputs.reshape(n_mat, rows, groups, cols).transpose(2, 1, 0, 3).reshape(groups, rows, n_mat * cols)
    norm_terms = norm_grads[0].astype(jnp.float32).reshape(n_mat, n_y, features).transpose(1, 0, 2)
    norm_terms = jnp.pad(norm_terms, ((0, 0), (0, rows - n_mat), (0, 0)))
    norm_terms = jnp.repeat(norm_terms, n_core, axis=0)
    sent = jnp.concatenate(
        [blocks, jnp.broadcast_to(own_factor[None], (groups, rows, n_mat * rank)), norm_terms], axis=2
    )
    lanes = sent.shape[2]
    at_factor, at_norm = n_mat * cols, n_mat * (cols + rank)
    got = lax.all_to_all(sent, ("y", "core"), 0, 0, tiled=True)
    over_y = jnp.sum(got.reshape(n_y, n_core, rows, lanes), axis=0)
    norm_y = lax.dynamic_index_in_dim(over_y, core, 0, keepdims=False)[:z_rows, at_norm:]
    norm_y = jnp.broadcast_to(norm_y[None], (n_z, z_rows, features))
    over_y = over_y.reshape(n_z, z_rows, lanes)
    sent = jnp.concatenate([over_y[:, :, :at_norm], norm_y], axis=2)
    got = lax.all_to_all(sent, "z", 0, 0, tiled=True)
    over_z = jnp.sum(got, axis=0)
    own_norm = lax.dynamic_slice(over_z, (0, at_norm + z * gain_cols), (n_mat, gain_cols))
    mean_norm = own_norm / replicas
    total = lax.all_gather(over_z, "z", axis=0, tiled=True)
    matrix = total[:, :at_factor].reshape(chip_rows, n_mat, cols).transpose(1, 0, 2)
    factor = total[:, at_factor:at_norm].reshape(chip_rows, n_mat, rank).transpose(1, 0, 2)

    def right_factor(factor):
        product = jnp.einsum("mrk,mrc->mkc", factor, matrix, precision=HIGH)
        gram = jnp.einsum("mrk,mrj->mkj", factor, factor, precision=HIGH)
        summed = jnp.sum(lax.all_gather(pack(product, gram), "x"), axis=0)
        product = jnp.stack([summed[:, m * cols : (m + 1) * cols] for m in range(n_mat)])
        start = n_mat * cols
        gram = jnp.stack([summed[:, start + m * rank : start + (m + 1) * rank] for m in range(n_mat)])
        triangle = jnp.linalg.cholesky(gram)
        return triangle, jax.vmap(tri_solve)(triangle, product)

    _, directions = right_factor(factor)
    factor = jnp.einsum("mrc,mkc->rmk", matrix, directions, precision=HIGH).reshape(n_core, rows, n_mat * rank)
    factor = factor.transpose(1, 0, 2).reshape(rows, n_core * n_mat * rank)
    factor = jnp.sum(spread(factor, ("y", "core"), groups), axis=0)
    factor = factor.reshape(rows, n_core, n_mat, rank).transpose(2, 1, 0, 3)
    triangle, directions = right_factor(factor.reshape(n_mat, chip_rows, rank))
    own_rows = lax.dynamic_index_in_dim(factor, core, 1, keepdims=False)
    basis_t = jax.vmap(tri_solve)(triangle, jnp.swapaxes(own_rows, 1, 2))
    directions = spread(directions, ("y", "core"), groups)
    directions = directions.transpose(1, 2, 0, 3).reshape(n_mat, rank, width)
    approx = jnp.einsum("mkr,mkd->mrd", basis_t, directions, precision=HIGH) / replicas
    new_error_kv = (inputs - approx).astype(jnp.bfloat16)[None]
    weight_cols = weight_kv.shape[2]
    own_dirs = lax.dynamic_slice_in_dim(directions, (y * n_z + z) * weight_cols, weight_cols, 2)
    own_approx = jnp.einsum("mkr,mkd->mrd", basis_t, own_dirs, precision=HIGH) / replicas
    new_weight_kv = weight_kv - step_size * own_approx
    new_gains = norm_gains - step_size * mean_norm[:, None, :]
    return (new_weight_kv, new_error_kv, new_moment_kv, new_gains)


def solution(mesh):
    dp, tensor = mesh.devices.shape
    sizes = (Y_CHIPS, dp // Y_CHIPS, tensor // CORES, CORES)
    chips = Mesh(mesh.devices.reshape(sizes), ("y", "z", "x", "core"))
    dp, tensor = ("y", "z"), ("x", "core")
    return jax.shard_map(
        shards,
        mesh=chips,
        in_specs=(
            P(dp, None, tensor, None),
            P(dp, None, tensor, None),
            P(dp, None, tensor, None),
            P(),
            P(None, tensor, dp),
            P(dp, None, tensor),
            P(None, tensor, dp),
        ),
        out_specs=(
            P(None, tensor, dp),
            P(dp, None, tensor, None),
            P(dp, None, tensor, None),
            P(None, tensor, dp),
        ),
        check_vma=False,
    )
```

```python
import functools

import jax
import jax.numpy as jnp
from jax import lax
from jax.experimental import pallas as pl
from jax.experimental.pallas import tpu as pltpu
from jax.sharding import Mesh
from jax.sharding import PartitionSpec as P

momentum_decay = 0.9
step_size = 0.5
Y_CHIPS = 4
CORES = 2
LANES = 128
PANEL = 4
STREAMS = ((0, 1),)
HIGH = lax.Precision.HIGHEST
F32 = jnp.float32


def dot(left, right, left_dim, right_dim):
    dims = (((left_dim,), (right_dim,)), ((), ()))
    return lax.dot_general(left, right, dims, precision=HIGH, preferred_element_type=F32)


def call(kernel, outs, *args, in_specs=None, out_specs=None, aliases=None):
    vmem = pl.BlockSpec(memory_space=pltpu.VMEM)
    return pl.pallas_call(
        kernel,
        out_shape=outs,
        in_specs=in_specs or [vmem] * len(args),
        out_specs=out_specs or jax.tree.map(lambda _: vmem, outs),
        input_output_aliases=aliases or {},
    )(*args)


def shape(*dims, dtype=F32):
    return jax.ShapeDtypeStruct(dims, dtype)


def iota(dims, axis):
    return lax.broadcasted_iota(jnp.int32, dims, axis)


def unrounded(moment, grad, error, m):
    moment_f = momentum_decay * moment[0, m].astype(F32) + grad[0, m].astype(F32)
    return moment_f + error[0, m].astype(F32)


def first_kernel(mats, groups, grad, error, moment, dirs, norm, sent):
    rows, width = grad.shape[2:]
    cols = width // groups
    rank = dirs.shape[1]
    at = len(mats) * cols
    sent[:, :, at:] = jnp.zeros((groups, rows, LANES), F32)
    for i, m in enumerate(mats):
        values = unrounded(moment, grad, error, m)
        for j in range(groups):
            sent[j, :, i * cols : (i + 1) * cols] = values[:, j * cols : (j + 1) * cols]
        factor = dot(values, dirs[m], 1, 1)
        for j in range(groups):
            sent[j, :, at + i * rank : at + (i + 1) * rank] = factor
    n_mat, per_tensor = norm.shape
    features = per_tensor // (groups // CORES)
    terms = norm[...].astype(F32)
    for j in range(groups):
        start = (j // CORES) * features
        sent[j, 0:n_mat, at + LANES // 2 : at + LANES // 2 + features] = terms[:, start : start + features]


def write_products(mats, cols, rank, matrix, factor, out):
    count = len(mats)
    grams = None
    lane = iota((rank, count * rank), 1)
    for i in range(count):
        own = factor[:, i * rank : (i + 1) * rank]
        product = dot(own, matrix[:, i * cols : (i + 1) * cols], 0, 0)
        gram = dot(own, factor, 0, 0)
        grams = gram if grams is None else jnp.where(lane >= i * rank, gram, grams)
        for j in range(out.shape[0]):
            out[j, :, i * cols : (i + 1) * cols] = product
    for j in range(out.shape[0]):
        out[j, :, count * cols :] = jnp.zeros((rank, LANES), F32)
        out[j, :, count * cols : count * (cols + rank)] = grams


def product_kernel(mats, cols, rank, matrix, out):
    count = len(mats)
    factor = matrix[:, count * cols : count * (cols + rank)]
    write_products(mats, cols, rank, matrix, factor, out)


def unpack_kernel(mats, cols, rank, matrix, got, out, factor_out):
    count = len(mats)
    summed = jnp.sum(got[...], axis=0)
    pieces = LANES // (count * rank)
    height = summed.shape[0]
    for j in range(pieces):
        factor_out[j * height : (j + 1) * height, :] = summed[:, j * count * rank : (j + 1) * count * rank]
    write_products(mats, cols, rank, matrix, factor_out[...], out)


def inverse_factors(a, count, rank):
    dims = a.shape
    row = iota(dims, 0)
    place = (iota(dims, 1) // rank) % count
    pivots = jnp.ones(dims, F32)
    for p in range(0, rank, PANEL):
        columns, lines = [], []
        for j in range(p, p + PANEL):
            column = jnp.broadcast_to(a[:, j : j + 1], dims)
            for i in range(1, count):
                other = jnp.broadcast_to(a[:, i * rank + j : i * rank + j + 1], dims)
                column = jnp.where(place == i, other, column)
            columns.append(column)
            lines.append(a[j : j + 1, :])
        for j in range(PANEL):
            pivot = columns[j][p + j : p + j + 1, :]
            times = jnp.where(row > p + j, columns[j], 0.0) * (1.0 / pivot)
            a = a - times * lines[j]
            pivots = jnp.where(row == p + j, pivot, pivots)
            for q in range(j + 1, PANEL):
                columns[q] = columns[q] - times * columns[j][p + q : p + q + 1, :]
                lines[q] = lines[q] - times[p + q : p + q + 1, :] * lines[j]
    scaled = a * (1.0 / jnp.sqrt(pivots))
    at = count * rank
    return [scaled[:, at + i * rank : at + (i + 1) * rank] for i in range(count)]


def solved(mats, cols, rank, got):
    count = len(mats)
    summed = jnp.sum(got[...], axis=0)
    a = summed[:, count * cols :]
    lane, row = iota(a.shape, 1), iota(a.shape, 0)
    at = count * rank
    one = (lane >= at) & (lane < 2 * at) & (lane % rank == row)
    inverses = inverse_factors(jnp.where(one, 1.0, a), count, rank)
    return inverses, [dot(inverses[i], summed[:, i * cols : (i + 1) * cols], 1, 0) for i in range(count)]


def left_kernel(mats, cols, rank, got, matrix, out):
    count = len(mats)
    _, directions = solved(mats, cols, rank, got)
    height = out.shape[1]
    for i in range(count):
        factor = dot(matrix[:, i * cols : (i + 1) * cols], directions[i], 1, 1)
        for piece in range(LANES // (count * rank)):
            part = factor[piece * height : (piece + 1) * height, :]
            start = (piece * count + i) * rank
            for j in range(out.shape[0]):
                out[j, :, start : start + rank] = part


def right_kernel(mats, cols, rank, rows, core, got, factor, out, basis):
    inverses, directions = solved(mats, cols, rank, got)
    start = pl.multiple_of(core[0] * rows, rows)
    own = factor[pl.ds(start, rows), :]
    for i in range(len(mats)):
        for j in range(out.shape[0]):
            out[j, i * rank : (i + 1) * rank, :] = directions[i]
        basis[i] = dot(own[:, i * rank : (i + 1) * rank], inverses[i], 1, 1)


def last_kernel(mats, replicas, rank, place, got, basis, grad, error, moment, weight, *refs):
    new_error, new_weight = refs[-2:]
    cols = got.shape[2]
    weight_cols = weight.shape[1]
    for i, m in enumerate(mats):
        values = unrounded(moment, grad, error, m)
        left = basis[i]
        for j in range(got.shape[0]):
            approx = dot(left, got[j, i * rank : (i + 1) * rank, :], 1, 0) / replicas
            part = values[:, j * cols : (j + 1) * cols] - approx
            new_error[0, i, :, j * cols : (j + 1) * cols] = part.astype(jnp.bfloat16)
        own = got[place[0], i * rank : (i + 1) * rank, :]
        own = pltpu.roll(own, place[1], 1)[:, :LANES]
        approx = dot(own, left, 0, 1) / replicas
        new_weight[i] = weight[m] - step_size * approx[:weight_cols, :]


def exchange(value, axes):
    return lax.all_to_all(value, axes, 0, 0, tiled=True)


def shards(grad_kv, error_kv, moment_kv, start_dirs, weight_kv, norm_grads, norm_gains):
    n_y, n_z, n_x, n_core = (lax.axis_size(a) for a in ("y", "z", "x", "core"))
    replicas = n_y * n_z
    y, z, core = (lax.axis_index(a) for a in ("y", "z", "core"))
    _, n_mat, rows, width = grad_kv.shape
    rank = start_dirs.shape[1]
    groups = n_y * n_core
    cols = width // groups
    chip_rows = rows * n_core
    z_rows = chip_rows // n_z
    gain_cols = norm_gains.shape[2]
    weight_cols = weight_kv.shape[2]
    weight_t = jnp.swapaxes(weight_kv, 1, 2)
    smem = pl.BlockSpec(memory_space=pltpu.SMEM)
    vmem = pl.BlockSpec(memory_space=pltpu.VMEM)
    core_at = core[None]
    column = (y * n_z + z) * weight_cols
    place = jnp.stack([column // cols, (cols - column % cols) % cols])

    moment_f = momentum_decay * moment_kv.astype(F32) + grad_kv.astype(F32)
    new_moment_kv = moment_f.astype(jnp.bfloat16)

    new_gains, errors, weights = None, [], []
    for mats in STREAMS:
        count = len(mats)
        lanes = count * cols + LANES
        at = count * cols
        norm_at = at + LANES // 2
        sent = call(
            functools.partial(first_kernel, mats, groups),
            shape(groups, rows, lanes),
            grad_kv, error_kv, moment_kv, start_dirs, norm_grads[0],
        )
        got = exchange(sent, ("y", "core"))
        over_y = jnp.sum(got.reshape(n_y, n_core, rows, lanes), axis=0)
        norm_y = lax.dynamic_index_in_dim(over_y, core, 0, keepdims=False)[:z_rows, norm_at:]
        norm_y = jnp.broadcast_to(norm_y[None], (n_z, z_rows, LANES // 2))
        sent = jnp.concatenate([over_y.reshape(n_z, z_rows, lanes)[:, :, :norm_at], norm_y], axis=2)
        over_z = jnp.sum(exchange(sent, "z"), axis=0)
        if new_gains is None:
            own_norm = lax.dynamic_slice(over_z, (0, norm_at + z * gain_cols), (n_mat, gain_cols))
            new_gains = norm_gains - step_size * (own_norm / replicas)[:, None, :]
        copies = jnp.broadcast_to(over_z[None], (n_z, z_rows, lanes))
        matrix = exchange(copies, "z").reshape(chip_rows, lanes)

        sizes = (mats, cols, rank)
        height = chip_rows * count * rank // LANES
        products = call(functools.partial(product_kernel, *sizes), shape(n_x, rank, lanes), matrix)
        got = exchange(products, "x")
        factors = call(functools.partial(left_kernel, *sizes), shape(groups, height, LANES), got, matrix)
        got = exchange(factors, ("y", "core"))
        products, factor = call(
            functools.partial(unpack_kernel, *sizes),
            (shape(n_x, rank, lanes), shape(chip_rows, count * rank)),
            matrix, got,
        )
        got = exchange(products, "x")
        directions, basis = call(
            functools.partial(right_kernel, *sizes, rows),
            (shape(groups, count * rank, cols), shape(count, rows, rank)),
            core_at, got, factor,
            in_specs=[smem, vmem, vmem],
        )
        got = exchange(directions, ("y", "core"))
        error, weight = call(
            functools.partial(last_kernel, mats, replicas, rank),
            (shape(1, count, rows, width, dtype=jnp.bfloat16), shape(count, weight_cols, rows)),
            place, got, basis, grad_kv, error_kv, moment_kv, weight_t,
            in_specs=[smem] + [vmem] * 6,
        )
        errors.append(error)
        weights.append(weight)
    new_error_kv = jnp.concatenate(errors, axis=1)
    new_weight_kv = jnp.swapaxes(jnp.concatenate(weights, axis=0), 1, 2)
    return (new_weight_kv, new_error_kv, new_moment_kv, new_gains)


def solution(mesh):
    dp, tensor = mesh.devices.shape
    sizes = (Y_CHIPS, dp // Y_CHIPS, tensor // CORES, CORES)
    chips = Mesh(mesh.devices.reshape(sizes), ("y", "z", "x", "core"))
    dp, tensor = ("y", "z"), ("x", "core")
    return jax.shard_map(
        shards,
        mesh=chips,
        in_specs=(
            P(dp, None, tensor, None),
            P(dp, None, tensor, None),
            P(dp, None, tensor, None),
            P(),
            P(None, tensor, dp),
            P(dp, None, tensor),
            P(None, tensor, dp),
        ),
        out_specs=(
            P(None, tensor, dp),
            P(dp, None, tensor, None),
            P(dp, None, tensor, None),
            P(None, tensor, dp),
        ),
        check_vma=False,
    )
```

```python
import functools

import jax
import jax.numpy as jnp
from jax import lax
from jax.experimental import pallas as pl
from jax.experimental.pallas import tpu as pltpu
from jax.sharding import Mesh
from jax.sharding import PartitionSpec as P

momentum_decay = 0.9
step_size = 0.5
Y_CHIPS = 4
CORES = 2
LANES = 128
PANEL = 4
STREAMS = ((0, 1),)
HIGH = lax.Precision.HIGHEST
F32 = jnp.float32


def dot(left, right, left_dim, right_dim):
    dims = (((left_dim,), (right_dim,)), ((), ()))
    return lax.dot_general(left, right, dims, precision=HIGH, preferred_element_type=F32)


def call(kernel, outs, *args, in_specs=None, out_specs=None, aliases=None):
    vmem = pl.BlockSpec(memory_space=pltpu.VMEM)
    return pl.pallas_call(
        kernel,
        out_shape=outs,
        in_specs=in_specs or [vmem] * len(args),
        out_specs=out_specs or jax.tree.map(lambda _: vmem, outs),
        input_output_aliases=aliases or {},
    )(*args)


def shape(*dims, dtype=F32):
    return jax.ShapeDtypeStruct(dims, dtype)


def local(*dims):
    return pltpu.VMEM(dims, F32)


def keep(value):
    return pltpu.with_memory_space_constraint(value, pltpu.VMEM)


def iota(dims, axis):
    return lax.broadcasted_iota(jnp.int32, dims, axis)


def unrounded(moment, grad, error, m):
    moment_f = momentum_decay * moment[0, m].astype(F32) + grad[0, m].astype(F32)
    return moment_f + error[0, m].astype(F32)


def first_kernel(mats, groups, grad, error, moment, dirs, norm, sent):
    rows, width = grad.shape[2:]
    cols = width // groups
    rank = dirs.shape[1]
    at = len(mats) * cols
    sent[:, :, at:] = jnp.zeros((groups, rows, LANES), F32)
    for i, m in enumerate(mats):
        values = unrounded(moment, grad, error, m)
        for j in range(groups):
            sent[j, :, i * cols : (i + 1) * cols] = values[:, j * cols : (j + 1) * cols]
        factor = dot(values, dirs[m], 1, 1)
        for j in range(groups):
            sent[j, :, at + i * rank : at + (i + 1) * rank] = factor
    n_mat, per_tensor = norm.shape
    features = per_tensor // (groups // CORES)
    terms = norm[...].astype(F32)
    for j in range(groups):
        start = (j // CORES) * features
        sent[j, 0:n_mat, at + LANES // 2 : at + LANES // 2 + features] = terms[:, start : start + features]


def write_products(mats, cols, rank, matrix, factor, out):
    count = len(mats)
    grams = None
    lane = iota((rank, count * rank), 1)
    for i in range(count):
        own = factor[:, i * rank : (i + 1) * rank]
        product = dot(own, matrix[:, i * cols : (i + 1) * cols], 0, 0)
        gram = dot(own, factor, 0, 0)
        grams = gram if grams is None else jnp.where(lane >= i * rank, gram, grams)
        for j in range(out.shape[0]):
            out[j, :, i * cols : (i + 1) * cols] = product
    for j in range(out.shape[0]):
        out[j, :, count * cols :] = jnp.zeros((rank, LANES), F32)
        out[j, :, count * cols : count * (cols + rank)] = grams


def product_kernel(mats, cols, rank, matrix, out):
    count = len(mats)
    factor = matrix[:, count * cols : count * (cols + rank)]
    write_products(mats, cols, rank, matrix, factor, out)


def unpack_kernel(mats, cols, rank, matrix, got, out, factor_out):
    count = len(mats)
    summed = jnp.sum(got[...], axis=0)
    pieces = LANES // (count * rank)
    height = summed.shape[0]
    for j in range(pieces):
        factor_out[j * height : (j + 1) * height, :] = summed[:, j * count * rank : (j + 1) * count * rank]
    write_products(mats, cols, rank, matrix, factor_out[...], out)


def inverse_factors(a, count, rank):
    dims = a.shape
    row = iota(dims, 0)
    place = (iota(dims, 1) // rank) % count
    pivots = jnp.ones(dims, F32)
    for p in range(0, rank, PANEL):
        columns, lines = [], []
        for j in range(p, p + PANEL):
            column = jnp.broadcast_to(a[:, j : j + 1], dims)
            for i in range(1, count):
                other = jnp.broadcast_to(a[:, i * rank + j : i * rank + j + 1], dims)
                column = jnp.where(place == i, other, column)
            columns.append(column)
            lines.append(a[j : j + 1, :])
        for j in range(PANEL):
            pivot = columns[j][p + j : p + j + 1, :]
            times = jnp.where(row > p + j, columns[j], 0.0) * (1.0 / pivot)
            a = a - times * lines[j]
            pivots = jnp.where(row == p + j, pivot, pivots)
            for q in range(j + 1, PANEL):
                columns[q] = columns[q] - times * columns[j][p + q : p + q + 1, :]
                lines[q] = lines[q] - times[p + q : p + q + 1, :] * lines[j]
    scaled = a * (1.0 / jnp.sqrt(pivots))
    at = count * rank
    return [scaled[:, at + i * rank : at + (i + 1) * rank] for i in range(count)]


def solved(mats, cols, rank, got):
    count = len(mats)
    summed = jnp.sum(got[...], axis=0)
    a = summed[:, count * cols :]
    lane, row = iota(a.shape, 1), iota(a.shape, 0)
    at = count * rank
    one = (lane >= at) & (lane < 2 * at) & (lane % rank == row)
    inverses = inverse_factors(jnp.where(one, 1.0, a), count, rank)
    return inverses, [dot(inverses[i], summed[:, i * cols : (i + 1) * cols], 1, 0) for i in range(count)]


def left_kernel(mats, cols, rank, got, matrix, out):
    count = len(mats)
    _, directions = solved(mats, cols, rank, got)
    height = out.shape[1]
    for i in range(count):
        factor = dot(matrix[:, i * cols : (i + 1) * cols], directions[i], 1, 1)
        for piece in range(LANES // (count * rank)):
            part = factor[piece * height : (piece + 1) * height, :]
            start = (piece * count + i) * rank
            for j in range(out.shape[0]):
                out[j, :, start : start + rank] = part


def right_kernel(mats, cols, rank, rows, core, got, factor, out, basis):
    inverses, directions = solved(mats, cols, rank, got)
    start = pl.multiple_of(core[0] * rows, rows)
    own = factor[pl.ds(start, rows), :]
    for i in range(len(mats)):
        for j in range(out.shape[0]):
            out[j, i * rank : (i + 1) * rank, :] = directions[i]
        basis[i] = dot(own[:, i * rank : (i + 1) * rank], inverses[i], 1, 1)


def last_kernel(mats, replicas, rank, place, got, basis, grad, error, moment, weight, *refs):
    new_error, new_weight = refs[-2:]
    cols = got.shape[2]
    weight_cols = weight.shape[1]
    for i, m in enumerate(mats):
        values = unrounded(moment, grad, error, m)
        left = basis[i]
        for j in range(got.shape[0]):
            approx = dot(left, got[j, i * rank : (i + 1) * rank, :], 1, 0) / replicas
            part = values[:, j * cols : (j + 1) * cols] - approx
            new_error[0, i, :, j * cols : (j + 1) * cols] = part.astype(jnp.bfloat16)
        own = got[place[0], i * rank : (i + 1) * rank, :]
        own = pltpu.roll(own, place[1], 1)[:, :LANES]
        approx = dot(own, left, 0, 1) / replicas
        new_weight[i] = weight[m] - step_size * approx[:weight_cols, :]


def exchange(value, axes):
    return keep(lax.all_to_all(value, axes, 0, 0, tiled=True))


def shards(grad_kv, error_kv, moment_kv, start_dirs, weight_kv, norm_grads, norm_gains):
    n_y, n_z, n_x, n_core = (lax.axis_size(a) for a in ("y", "z", "x", "core"))
    replicas = n_y * n_z
    y, z, core = (lax.axis_index(a) for a in ("y", "z", "core"))
    _, n_mat, rows, width = grad_kv.shape
    rank = start_dirs.shape[1]
    groups = n_y * n_core
    cols = width // groups
    chip_rows = rows * n_core
    z_rows = chip_rows // n_z
    gain_cols = norm_gains.shape[2]
    weight_cols = weight_kv.shape[2]
    weight_t = jnp.swapaxes(weight_kv, 1, 2)
    smem = pl.BlockSpec(memory_space=pltpu.SMEM)
    vmem = pl.BlockSpec(memory_space=pltpu.VMEM)
    core_at = core[None]
    column = (y * n_z + z) * weight_cols
    place = jnp.stack([column // cols, (cols - column % cols) % cols])

    moment_f = momentum_decay * moment_kv.astype(F32) + grad_kv.astype(F32)
    new_moment_kv = moment_f.astype(jnp.bfloat16)

    new_gains, errors, weights = None, [], []
    for mats in STREAMS:
        count = len(mats)
        lanes = count * cols + LANES
        at = count * cols
        norm_at = at + LANES // 2
        sent = call(
            functools.partial(first_kernel, mats, groups),
            local(groups, rows, lanes),
            grad_kv, error_kv, moment_kv, start_dirs, norm_grads[0],
        )
        got = lax.all_to_all(sent, ("y", "core"), 0, 0, tiled=True)
        over_y = jnp.sum(got.reshape(n_y, n_core, rows, lanes), axis=0)
        norm_y = lax.dynamic_index_in_dim(over_y, core, 0, keepdims=False)[:z_rows, norm_at:]
        norm_y = jnp.broadcast_to(norm_y[None], (n_z, z_rows, LANES // 2))
        sent = jnp.concatenate([over_y.reshape(n_z, z_rows, lanes)[:, :, :norm_at], norm_y], axis=2)
        over_z = jnp.sum(lax.all_to_all(sent, "z", 0, 0, tiled=True), axis=0)
        if new_gains is None:
            own_norm = lax.dynamic_slice(over_z, (0, norm_at + z * gain_cols), (n_mat, gain_cols))
            new_gains = norm_gains - step_size * (own_norm / replicas)[:, None, :]
        copies = jnp.broadcast_to(over_z[None], (n_z, z_rows, lanes))
        matrix = lax.all_to_all(copies, "z", 0, 0, tiled=True)
        matrix = keep(matrix.reshape(chip_rows, lanes))

        sizes = (mats, cols, rank)
        height = chip_rows * count * rank // LANES
        products = call(functools.partial(product_kernel, *sizes), local(n_x, rank, lanes), matrix)
        got = exchange(products, "x")
        factors = call(functools.partial(left_kernel, *sizes), local(groups, height, LANES), got, matrix)
        got = exchange(factors, ("y", "core"))
        products, factor = call(
            functools.partial(unpack_kernel, *sizes),
            (local(n_x, rank, lanes), local(chip_rows, count * rank)),
            matrix, got,
        )
        got = exchange(products, "x")
        directions, basis = call(
            functools.partial(right_kernel, *sizes, rows),
            (local(groups, count * rank, cols), local(count, rows, rank)),
            core_at, got, keep(factor),
            in_specs=[smem, vmem, vmem],
        )
        got = exchange(directions, ("y", "core"))
        error, weight = call(
            functools.partial(last_kernel, mats, replicas, rank),
            (shape(1, count, rows, width, dtype=jnp.bfloat16), shape(count, weight_cols, rows)),
            place, got, keep(basis), grad_kv, error_kv, moment_kv, weight_t,
            in_specs=[smem] + [vmem] * 6,
        )
        errors.append(error)
        weights.append(weight)
    new_error_kv = jnp.concatenate(errors, axis=1)
    new_weight_kv = jnp.swapaxes(jnp.concatenate(weights, axis=0), 1, 2)
    return (new_weight_kv, new_error_kv, new_moment_kv, new_gains)


def solution(mesh):
    dp, tensor = mesh.devices.shape
    sizes = (Y_CHIPS, dp // Y_CHIPS, tensor // CORES, CORES)
    chips = Mesh(mesh.devices.reshape(sizes), ("y", "z", "x", "core"))
    dp, tensor = ("y", "z"), ("x", "core")
    return jax.shard_map(
        shards,
        mesh=chips,
        in_specs=(
            P(dp, None, tensor, None),
            P(dp, None, tensor, None),
            P(dp, None, tensor, None),
            P(),
            P(None, tensor, dp),
            P(dp, None, tensor),
            P(None, tensor, dp),
        ),
        out_specs=(
            P(None, tensor, dp),
            P(dp, None, tensor, None),
            P(dp, None, tensor, None),
            P(None, tensor, dp),
        ),
        check_vma=False,
    )
```

```python
import functools

import jax
import jax.numpy as jnp
from jax import lax
from jax.experimental import pallas as pl
from jax.experimental.pallas import tpu as pltpu
from jax.sharding import Mesh
from jax.sharding import PartitionSpec as P

momentum_decay = 0.9
step_size = 0.5
Y_CHIPS = 4
CORES = 2
PAIR = 2
LANES = 128
PANEL = 4
STREAMS = ((0, 1),)
HIGH = lax.Precision.HIGHEST
F32 = jnp.float32


def dot(left, right, left_dim, right_dim):
    dims = (((left_dim,), (right_dim,)), ((), ()))
    return lax.dot_general(left, right, dims, precision=HIGH, preferred_element_type=F32)


def call(kernel, outs, *args, in_specs=None, out_specs=None, aliases=None):
    vmem = pl.BlockSpec(memory_space=pltpu.VMEM)
    return pl.pallas_call(
        kernel,
        out_shape=outs,
        in_specs=in_specs or [vmem] * len(args),
        out_specs=out_specs or jax.tree.map(lambda _: vmem, outs),
        input_output_aliases=aliases or {},
    )(*args)


def shape(*dims, dtype=F32):
    return jax.ShapeDtypeStruct(dims, dtype)


def local(*dims):
    return pltpu.VMEM(dims, F32)


def keep(value):
    return pltpu.with_memory_space_constraint(value, pltpu.VMEM)


def iota(dims, axis):
    return lax.broadcasted_iota(jnp.int32, dims, axis)


def unrounded(moment, grad, error, m):
    moment_f = momentum_decay * moment[0, m].astype(F32) + grad[0, m].astype(F32)
    return moment_f + error[0, m].astype(F32)


def first_kernel(mats, groups, block, grad, error, moment, dirs, norm, sent):
    rows, width = grad.shape[2:]
    cols = width // groups
    rank = dirs.shape[1]
    at = len(mats) * cols
    total, height = sent.shape[:2]
    sent[:, :, at:] = jnp.zeros((total, height, LANES), F32)
    places = [(j, zl, q) for j in range(groups) for zl in range(PAIR) for q in range(height // block)]

    def dest(j, zl):
        return (j // CORES * PAIR + zl) * CORES + j % CORES

    for i, m in enumerate(mats):
        values = unrounded(moment, grad, error, m)
        factor = dot(values, dirs[m], 1, 1)
        for j, zl, q in places:
            start = (q * PAIR + zl) * block
            own = slice(q * block, (q + 1) * block)
            sent[dest(j, zl), own, i * cols : (i + 1) * cols] = values[start : start + block, j * cols : (j + 1) * cols]
            sent[dest(j, zl), own, at + i * rank : at + (i + 1) * rank] = factor[start : start + block, :]
    n_mat, per_tensor = norm.shape
    features = per_tensor // (groups // CORES)
    terms = norm[...].astype(F32)
    for j in range(groups):
        start = (j // CORES) * features
        for zl in range(PAIR):
            lane = at + LANES // 2
            sent[dest(j, zl), 0:n_mat, lane : lane + features] = terms[:, start : start + features]


def write_products(mats, cols, rank, matrix, factor, out):
    count = len(mats)
    grams = None
    lane = iota((rank, count * rank), 1)
    for i in range(count):
        own = factor[:, i * rank : (i + 1) * rank]
        product = dot(own, matrix[:, i * cols : (i + 1) * cols], 0, 0)
        gram = dot(own, factor, 0, 0)
        grams = gram if grams is None else jnp.where(lane >= i * rank, gram, grams)
        for j in range(out.shape[0]):
            out[j, :, i * cols : (i + 1) * cols] = product
    for j in range(out.shape[0]):
        out[j, :, count * cols :] = jnp.zeros((rank, LANES), F32)
        out[j, :, count * cols : count * (cols + rank)] = grams


def product_kernel(mats, cols, rank, matrix, out):
    count = len(mats)
    factor = matrix[:, count * cols : count * (cols + rank)]
    write_products(mats, cols, rank, matrix, factor, out)


def unpack_kernel(mats, cols, rank, matrix, got, out, factor_out):
    count = len(mats)
    summed = jnp.sum(got[...], axis=0)
    pieces = LANES // (count * rank)
    height = summed.shape[0]
    for j in range(pieces):
        factor_out[j * height : (j + 1) * height, :] = summed[:, j * count * rank : (j + 1) * count * rank]
    write_products(mats, cols, rank, matrix, factor_out[...], out)


def inverse_factors(a, count, rank):
    dims = a.shape
    row = iota(dims, 0)
    place = (iota(dims, 1) // rank) % count
    pivots = jnp.ones(dims, F32)
    for p in range(0, rank, PANEL):
        columns, lines = [], []
        for j in range(p, p + PANEL):
            column = jnp.broadcast_to(a[:, j : j + 1], dims)
            for i in range(1, count):
                other = jnp.broadcast_to(a[:, i * rank + j : i * rank + j + 1], dims)
                column = jnp.where(place == i, other, column)
            columns.append(column)
            lines.append(a[j : j + 1, :])
        for j in range(PANEL):
            pivot = columns[j][p + j : p + j + 1, :]
            times = jnp.where(row > p + j, columns[j], 0.0) * (1.0 / pivot)
            a = a - times * lines[j]
            pivots = jnp.where(row == p + j, pivot, pivots)
            for q in range(j + 1, PANEL):
                columns[q] = columns[q] - times * columns[j][p + q : p + q + 1, :]
                lines[q] = lines[q] - times[p + q : p + q + 1, :] * lines[j]
    scaled = a * (1.0 / jnp.sqrt(pivots))
    at = count * rank
    return [scaled[:, at + i * rank : at + (i + 1) * rank] for i in range(count)]


def solved(mats, cols, rank, got):
    count = len(mats)
    summed = jnp.sum(got[...], axis=0)
    a = summed[:, count * cols :]
    lane, row = iota(a.shape, 1), iota(a.shape, 0)
    at = count * rank
    one = (lane >= at) & (lane < 2 * at) & (lane % rank == row)
    inverses = inverse_factors(jnp.where(one, 1.0, a), count, rank)
    return inverses, [dot(inverses[i], summed[:, i * cols : (i + 1) * cols], 1, 0) for i in range(count)]


def left_kernel(mats, cols, rank, got, matrix, out):
    count = len(mats)
    _, directions = solved(mats, cols, rank, got)
    height = out.shape[1]
    for i in range(count):
        factor = dot(matrix[:, i * cols : (i + 1) * cols], directions[i], 1, 1)
        for piece in range(LANES // (count * rank)):
            part = factor[piece * height : (piece + 1) * height, :]
            start = (piece * count + i) * rank
            for j in range(out.shape[0]):
                out[j, :, start : start + rank] = part


def right_kernel(mats, cols, rank, rows, core, got, factor, out, basis):
    inverses, directions = solved(mats, cols, rank, got)
    start = pl.multiple_of(core[0] * rows, rows)
    own = factor[pl.ds(start, rows), :]
    for i in range(len(mats)):
        for j in range(out.shape[0]):
            out[j, i * rank : (i + 1) * rank, :] = directions[i]
        basis[i] = dot(own[:, i * rank : (i + 1) * rank], inverses[i], 1, 1)


def last_kernel(mats, replicas, rank, place, got, other, basis, grad, error, moment, weight, new_error, new_weight):
    cols = got.shape[2]
    weight_cols = weight.shape[1]
    first, same = place[2] == 0, place[3] == 1
    for i, m in enumerate(mats):
        values = unrounded(moment, grad, error, m)
        left = basis[i]
        own_rank = slice(i * rank, (i + 1) * rank)
        for y in range(got.shape[0]):
            mine, theirs = got[y, own_rank, :], other[y, own_rank, :]
            for c in range(CORES):
                right = jnp.where(first, *((mine, theirs) if c == 0 else (theirs, mine)))
                approx = dot(left, right, 1, 0) / replicas
                start = (y * CORES + c) * cols
                part = values[:, start : start + cols] - approx
                new_error[0, i, :, start : start + cols] = part.astype(jnp.bfloat16)
        own = jnp.where(same, got[place[0], own_rank, :], other[place[0], own_rank, :])
        own = pltpu.roll(own, place[1], 1)[:, :LANES]
        approx = dot(own, left, 0, 1) / replicas
        new_weight[i] = weight[m] - step_size * approx[:weight_cols, :]


def exchange(value, axes):
    return keep(lax.all_to_all(value, axes, 0, 0, tiled=True))


def shards(grad_kv, error_kv, moment_kv, start_dirs, weight_kv, norm_grads, norm_gains):
    n_y, n_zh, n_zl, n_x, n_core = (lax.axis_size(a) for a in ("y", "zh", "zl", "x", "core"))
    n_z = n_zh * n_zl
    replicas = n_y * n_z
    y, core = lax.axis_index("y"), lax.axis_index("core")
    z = lax.axis_index("zh") * n_zl + lax.axis_index("zl")
    _, n_mat, rows, width = grad_kv.shape
    rank = start_dirs.shape[1]
    groups = n_y * n_core
    cols = width // groups
    chip_rows = rows * n_core
    z_rows = chip_rows // n_z
    gain_cols = norm_gains.shape[2]
    weight_cols = weight_kv.shape[2]
    weight_t = jnp.swapaxes(weight_kv, 1, 2)
    smem = pl.BlockSpec(memory_space=pltpu.SMEM)
    vmem = pl.BlockSpec(memory_space=pltpu.VMEM)
    core_at = core[None]
    column = (y * n_z + z) * weight_cols
    group = column // cols
    same = (group % n_core == core).astype(jnp.int32)
    place = jnp.stack([group // n_core, (cols - column % cols) % cols, core, same])

    moment_f = momentum_decay * moment_kv.astype(F32) + grad_kv.astype(F32)
    new_moment_kv = moment_f.astype(jnp.bfloat16)

    new_gains, errors, weights = None, [], []
    for mats in STREAMS:
        count = len(mats)
        lanes = count * cols + LANES
        at = count * cols
        norm_at = at + LANES // 2
        sent = call(
            functools.partial(first_kernel, mats, groups, z_rows),
            local(groups * n_zl, rows // n_zl, lanes),
            grad_kv, error_kv, moment_kv, start_dirs, norm_grads[0],
        )
        got = lax.all_to_all(sent, ("y", "zl", "core"), 0, 0, tiled=True)
        over_y = jnp.sum(got.reshape(n_y * n_zl, n_core, rows // n_zl, lanes), axis=0)
        norm_y = lax.dynamic_index_in_dim(over_y, core, 0, keepdims=False)[:z_rows, norm_at:]
        norm_y = jnp.broadcast_to(norm_y[None], (n_zh, z_rows, LANES // 2))
        sent = jnp.concatenate([over_y.reshape(n_zh, z_rows, lanes)[:, :, :norm_at], norm_y], axis=2)
        over_z = jnp.sum(lax.all_to_all(sent, "zh", 0, 0, tiled=True), axis=0)
        if new_gains is None:
            own_norm = lax.dynamic_slice(over_z, (0, norm_at + z * gain_cols), (n_mat, gain_cols))
            new_gains = norm_gains - step_size * (own_norm / replicas)[:, None, :]
        copies = jnp.broadcast_to(over_z[None], (n_z, z_rows, lanes))
        matrix = lax.all_to_all(copies, ("zh", "zl"), 0, 0, tiled=True)
        matrix = keep(matrix.reshape(chip_rows, lanes))

        sizes = (mats, cols, rank)
        height = chip_rows * count * rank // LANES
        products = call(functools.partial(product_kernel, *sizes), local(n_x, rank, lanes), matrix)
        got = exchange(products, "x")
        factors = call(functools.partial(left_kernel, *sizes), local(groups, height, LANES), got, matrix)
        got = exchange(factors, ("y", "core"))
        products, factor = call(
            functools.partial(unpack_kernel, *sizes),
            (local(n_x, rank, lanes), local(chip_rows, count * rank)),
            matrix, got,
        )
        got = exchange(products, "x")
        directions, basis = call(
            functools.partial(right_kernel, *sizes, rows),
            (local(n_y, count * rank, cols), local(count, rows, rank)),
            core_at, got, keep(factor),
            in_specs=[smem, vmem, vmem],
        )
        got = exchange(directions, "y")
        other = keep(lax.ppermute(got, "core", [(i, n_core - 1 - i) for i in range(n_core)]))
        error, weight = call(
            functools.partial(last_kernel, mats, replicas, rank),
            (shape(1, count, rows, width, dtype=jnp.bfloat16), shape(count, weight_cols, rows)),
            place, got, other, keep(basis), keep(grad_kv), keep(error_kv), keep(moment_kv), weight_t,
            in_specs=[smem] + [vmem] * 7,
        )
        errors.append(error)
        weights.append(weight)
    new_error_kv = jnp.concatenate(errors, axis=1)
    new_weight_kv = jnp.swapaxes(jnp.concatenate(weights, axis=0), 1, 2)
    return (new_weight_kv, new_error_kv, new_moment_kv, new_gains)


def solution(mesh):
    dp, tensor = mesh.devices.shape
    sizes = (Y_CHIPS, dp // Y_CHIPS // PAIR, PAIR, tensor // CORES, CORES)
    chips = Mesh(mesh.devices.reshape(sizes), ("y", "zh", "zl", "x", "core"))
    dp, tensor = ("y", "zh", "zl"), ("x", "core")
    return jax.shard_map(
        shards,
        mesh=chips,
        in_specs=(
            P(dp, None, tensor, None),
            P(dp, None, tensor, None),
            P(dp, None, tensor, None),
            P(),
            P(None, tensor, dp),
            P(dp, None, tensor),
            P(None, tensor, dp),
        ),
        out_specs=(
            P(None, tensor, dp),
            P(dp, None, tensor, None),
            P(dp, None, tensor, None),
            P(None, tensor, dp),
        ),
        check_vma=False,
    )
```

```python
import functools

import jax
import jax.numpy as jnp
from jax import lax
from jax.experimental import pallas as pl
from jax.experimental.pallas import tpu as pltpu
from jax.sharding import Mesh
from jax.sharding import PartitionSpec as P

momentum_decay = 0.9
step_size = 0.5
Y_CHIPS = 4
CORES = 2
PAIR = 2
LANES = 128
PANEL = 4
STREAMS = ((0, 1),)
HIGH = lax.Precision.HIGHEST
F32 = jnp.float32


def dot(left, right, left_dim, right_dim):
    dims = (((left_dim,), (right_dim,)), ((), ()))
    return lax.dot_general(left, right, dims, precision=HIGH, preferred_element_type=F32)


def call(kernel, outs, *args, in_specs=None, out_specs=None, aliases=None):
    vmem = pl.BlockSpec(memory_space=pltpu.VMEM)
    return pl.pallas_call(
        kernel,
        out_shape=outs,
        in_specs=in_specs or [vmem] * len(args),
        out_specs=out_specs or jax.tree.map(lambda _: vmem, outs),
        input_output_aliases=aliases or {},
    )(*args)


def shape(*dims, dtype=F32):
    return jax.ShapeDtypeStruct(dims, dtype)


def local(*dims):
    return pltpu.VMEM(dims, F32)


def keep(value):
    return pltpu.with_memory_space_constraint(value, pltpu.VMEM)


def iota(dims, axis):
    return lax.broadcasted_iota(jnp.int32, dims, axis)


def unrounded(moment, grad, error, m):
    moment_f = momentum_decay * moment[0, m].astype(F32) + grad[0, m].astype(F32)
    return moment_f + error[0, m].astype(F32)


def first_kernel(mats, groups, block, grad, error, moment, dirs, norm, sent):
    rows, width = grad.shape[2:]
    cols = width // groups
    rank = dirs.shape[1]
    at = len(mats) * cols
    total, height = sent.shape[:2]
    sent[:, :, at:] = jnp.zeros((total, height, LANES), F32)
    places = [(j, zl, q) for j in range(groups) for zl in range(PAIR) for q in range(height // block)]

    def dest(j, zl):
        return (j // CORES * PAIR + zl) * CORES + j % CORES

    for i, m in enumerate(mats):
        values = unrounded(moment, grad, error, m)
        factor = dot(values, dirs[m], 1, 1)
        for j, zl, q in places:
            start = (q * PAIR + zl) * block
            own = slice(q * block, (q + 1) * block)
            sent[dest(j, zl), own, i * cols : (i + 1) * cols] = values[start : start + block, j * cols : (j + 1) * cols]
            sent[dest(j, zl), own, at + i * rank : at + (i + 1) * rank] = factor[start : start + block, :]
    n_mat, per_tensor = norm.shape
    features = per_tensor // (groups // CORES)
    terms = norm[...].astype(F32)
    for j in range(groups):
        start = (j // CORES) * features
        for zl in range(PAIR):
            lane = at + LANES // 2
            sent[dest(j, zl), 0:n_mat, lane : lane + features] = terms[:, start : start + features]


def write_products(mats, cols, rank, matrix, factor, out):
    count = len(mats)
    grams = None
    lane = iota((rank, count * rank), 1)
    for i in range(count):
        own = factor[:, i * rank : (i + 1) * rank]
        product = dot(own, matrix[:, i * cols : (i + 1) * cols], 0, 0)
        gram = dot(own, factor, 0, 0)
        grams = gram if grams is None else jnp.where(lane >= i * rank, gram, grams)
        for j in range(out.shape[0]):
            out[j, :, i * cols : (i + 1) * cols] = product
    for j in range(out.shape[0]):
        out[j, :, count * cols :] = jnp.zeros((rank, LANES), F32)
        out[j, :, count * cols : count * (cols + rank)] = grams


def product_kernel(mats, cols, rank, matrix, out):
    count = len(mats)
    factor = matrix[:, count * cols : count * (cols + rank)]
    write_products(mats, cols, rank, matrix, factor, out)


def unpack_kernel(mats, cols, rank, matrix, got, out, factor_out):
    count = len(mats)
    summed = jnp.sum(got[...], axis=0)
    pieces = LANES // (count * rank)
    height = summed.shape[0]
    for j in range(pieces):
        factor_out[j * height : (j + 1) * height, :] = summed[:, j * count * rank : (j + 1) * count * rank]
    write_products(mats, cols, rank, matrix, factor_out[...], out)


def inverse_factors(a, count, rank):
    dims = a.shape
    row = iota(dims, 0)
    place = (iota(dims, 1) // rank) % count
    pivots = jnp.ones(dims, F32)
    for p in range(0, rank, PANEL):
        columns, lines = [], []
        for j in range(p, p + PANEL):
            column = jnp.broadcast_to(a[:, j : j + 1], dims)
            for i in range(1, count):
                other = jnp.broadcast_to(a[:, i * rank + j : i * rank + j + 1], dims)
                column = jnp.where(place == i, other, column)
            columns.append(column)
            lines.append(a[j : j + 1, :])
        for j in range(PANEL):
            pivot = columns[j][p + j : p + j + 1, :]
            times = jnp.where(row > p + j, columns[j], 0.0) * (1.0 / pivot)
            a = a - times * lines[j]
            pivots = jnp.where(row == p + j, pivot, pivots)
            for q in range(j + 1, PANEL):
                columns[q] = columns[q] - times * columns[j][p + q : p + q + 1, :]
                lines[q] = lines[q] - times[p + q : p + q + 1, :] * lines[j]
    scaled = a * (1.0 / jnp.sqrt(pivots))
    at = count * rank
    return [scaled[:, at + i * rank : at + (i + 1) * rank] for i in range(count)]


def solved(mats, cols, rank, got):
    count = len(mats)
    summed = jnp.sum(got[...], axis=0)
    a = summed[:, count * cols :]
    lane, row = iota(a.shape, 1), iota(a.shape, 0)
    at = count * rank
    one = (lane >= at) & (lane < 2 * at) & (lane % rank == row)
    inverses = inverse_factors(jnp.where(one, 1.0, a), count, rank)
    return inverses, [dot(inverses[i], summed[:, i * cols : (i + 1) * cols], 1, 0) for i in range(count)]


def left_kernel(mats, cols, rank, got, matrix, out):
    count = len(mats)
    _, directions = solved(mats, cols, rank, got)
    height = out.shape[1]
    for i in range(count):
        factor = dot(matrix[:, i * cols : (i + 1) * cols], directions[i], 1, 1)
        for piece in range(LANES // (count * rank)):
            part = factor[piece * height : (piece + 1) * height, :]
            start = (piece * count + i) * rank
            for j in range(out.shape[0]):
                out[j, :, start : start + rank] = part


def right_kernel(mats, cols, rank, rows, core, got, factor, out, basis):
    inverses, directions = solved(mats, cols, rank, got)
    start = pl.multiple_of(core[0] * rows, rows)
    own = factor[pl.ds(start, rows), :]
    for i in range(len(mats)):
        for j in range(out.shape[0]):
            out[j, i * rank : (i + 1) * rank, :] = directions[i]
        basis[i] = dot(own[:, i * rank : (i + 1) * rank], inverses[i], 1, 1)


def last_kernel(mats, replicas, rank, place, got, other, basis, grad, error, moment, weight, new_error, new_weight):
    cols = got.shape[2]
    weight_cols = weight.shape[1]
    first, same = place[2] == 0, place[3] == 1
    for i, m in enumerate(mats):
        values = unrounded(moment, grad, error, m)
        left = basis[i]
        own_rank = slice(i * rank, (i + 1) * rank)
        for y in range(got.shape[0]):
            mine, theirs = got[y, own_rank, :], other[y, own_rank, :]
            for c in range(CORES):
                right = jnp.where(first, *((mine, theirs) if c == 0 else (theirs, mine)))
                approx = dot(left, right, 1, 0) / replicas
                start = (y * CORES + c) * cols
                part = values[:, start : start + cols] - approx
                new_error[0, i, :, start : start + cols] = part.astype(jnp.bfloat16)
        own = jnp.where(same, got[place[0], own_rank, :], other[place[0], own_rank, :])
        own = pltpu.roll(own, place[1], 1)[:, :LANES]
        approx = dot(own, left, 0, 1) / replicas
        new_weight[i] = weight[m] - step_size * approx[:weight_cols, :]


def exchange(value, axes):
    return keep(lax.all_to_all(value, axes, 0, 0, tiled=True))


def shards(grad_kv, error_kv, moment_kv, start_dirs, weight_kv, norm_grads, norm_gains):
    n_y, n_zh, n_zl, n_x, n_core = (lax.axis_size(a) for a in ("y", "zh", "zl", "x", "core"))
    n_z = n_zh * n_zl
    replicas = n_y * n_z
    y, core = lax.axis_index("y"), lax.axis_index("core")
    z = lax.axis_index("zh") * n_zl + lax.axis_index("zl")
    _, n_mat, rows, width = grad_kv.shape
    rank = start_dirs.shape[1]
    groups = n_y * n_core
    cols = width // groups
    chip_rows = rows * n_core
    z_rows = chip_rows // n_z
    gain_cols = norm_gains.shape[2]
    weight_cols = weight_kv.shape[2]
    weight_t = jnp.swapaxes(weight_kv, 1, 2)
    smem = pl.BlockSpec(memory_space=pltpu.SMEM)
    vmem = pl.BlockSpec(memory_space=pltpu.VMEM)
    moment_f = momentum_decay * moment_kv.astype(F32) + grad_kv.astype(F32)
    new_moment_kv = moment_f.astype(jnp.bfloat16)

    new_gains, errors, weights = None, [], []
    for mats in STREAMS:
        count = len(mats)
        lanes = count * cols + LANES
        at = count * cols
        norm_at = at + LANES // 2
        sent = call(
            functools.partial(first_kernel, mats, groups, z_rows),
            local(groups * n_zl, rows // n_zl, lanes),
            grad_kv, error_kv, moment_kv, start_dirs, norm_grads[0],
        )
        sent, indices = lax.optimization_barrier((sent, (y, z, core)))
        got = lax.all_to_all(sent, ("y", "zl", "core"), 0, 0, tiled=True)
        got, (y, z, core) = lax.optimization_barrier((got, indices))
        core_at = core[None]
        column = (y * n_z + z) * weight_cols
        group = column // cols
        same = (group % n_core == core).astype(jnp.int32)
        place = jnp.stack([group // n_core, (cols - column % cols) % cols, core, same])
        over_y = jnp.sum(got.reshape(n_y * n_zl, n_core, rows // n_zl, lanes), axis=0)
        norm_y = lax.dynamic_index_in_dim(over_y, core, 0, keepdims=False)[:z_rows, norm_at:]
        norm_y = jnp.broadcast_to(norm_y[None], (n_zh, z_rows, LANES // 2))
        sent = jnp.concatenate([over_y.reshape(n_zh, z_rows, lanes)[:, :, :norm_at], norm_y], axis=2)
        over_z = jnp.sum(lax.all_to_all(sent, "zh", 0, 0, tiled=True), axis=0)
        if new_gains is None:
            own_norm = lax.dynamic_slice(over_z, (0, norm_at + z * gain_cols), (n_mat, gain_cols))
            new_gains = norm_gains - step_size * (own_norm / replicas)[:, None, :]
        copies = jnp.broadcast_to(over_z[None], (n_z, z_rows, lanes))
        matrix = lax.all_to_all(copies, ("zh", "zl"), 0, 0, tiled=True)
        matrix = keep(matrix.reshape(chip_rows, lanes))

        sizes = (mats, cols, rank)
        height = chip_rows * count * rank // LANES
        products = call(functools.partial(product_kernel, *sizes), local(n_x, rank, lanes), matrix)
        got = exchange(products, "x")
        factors = call(functools.partial(left_kernel, *sizes), local(groups, height, LANES), got, matrix)
        got = exchange(factors, ("y", "core"))
        products, factor = call(
            functools.partial(unpack_kernel, *sizes),
            (local(n_x, rank, lanes), local(chip_rows, count * rank)),
            matrix, got,
        )
        got = exchange(products, "x")
        directions, basis = call(
            functools.partial(right_kernel, *sizes, rows),
            (local(n_y, count * rank, cols), local(count, rows, rank)),
            core_at, got, keep(factor),
            in_specs=[smem, vmem, vmem],
        )
        got = exchange(directions, "y")
        other = keep(lax.ppermute(got, "core", [(i, n_core - 1 - i) for i in range(n_core)]))
        error, weight = call(
            functools.partial(last_kernel, mats, replicas, rank),
            (shape(1, count, rows, width, dtype=jnp.bfloat16), shape(count, weight_cols, rows)),
            place, got, other, keep(basis), keep(grad_kv), keep(error_kv), keep(moment_kv), weight_t,
            in_specs=[smem] + [vmem] * 7,
        )
        errors.append(error)
        weights.append(weight)
    new_error_kv = jnp.concatenate(errors, axis=1)
    new_weight_kv = jnp.swapaxes(jnp.concatenate(weights, axis=0), 1, 2)
    return (new_weight_kv, new_error_kv, new_moment_kv, new_gains)


def solution(mesh):
    dp, tensor = mesh.devices.shape
    sizes = (Y_CHIPS, dp // Y_CHIPS // PAIR, PAIR, tensor // CORES, CORES)
    chips = Mesh(mesh.devices.reshape(sizes), ("y", "zh", "zl", "x", "core"))
    dp, tensor = ("y", "zh", "zl"), ("x", "core")
    return jax.shard_map(
        shards,
        mesh=chips,
        in_specs=(
            P(dp, None, tensor, None),
            P(dp, None, tensor, None),
            P(dp, None, tensor, None),
            P(),
            P(None, tensor, dp),
            P(dp, None, tensor),
            P(None, tensor, dp),
        ),
        out_specs=(
            P(None, tensor, dp),
            P(dp, None, tensor, None),
            P(dp, None, tensor, None),
            P(None, tensor, dp),
        ),
        check_vma=False,
    )
```
